256 devices in a mesh: section: 4 (over x), tensor: 64 (over y, z, core).
Axes of the slice: x: 4, y: 4, z: 8, core: 2. Of those that a mesh axis runs over, the one named last changes fastest.
Arguments:
- hidden: bfloat16 [512, 16384], P('section', 'tensor')
- norm_gain: float32 [16384], P('tensor'), may hold values from 0.3 to 3
- head_weight: bfloat16 [16384, 65536], P(None, ('section', 'tensor'))
- tile_list: int32 [512, 128], replicated, may hold values from 0 to 511, as said below
- tile_count: int32 [512], replicated, may hold values from 1 to 128, as said below
- chosen_token: int32 [512], replicated, may hold values from 0 to 65535, as said below
- chosen_embed: bfloat16 [512, 16384], P('section', 'tensor'), may hold values from -6 to 6
- stack_state: int32 [512], P('section'), may hold values from 0 to 511
- state_table: bfloat16 [512, 16384], P(None, 'tensor'), may hold values from -6 to 6
Outputs:
- log_prob: float32 [512], replicated
- normalizer: float32 [512], replicated
- next_input: bfloat16 [512, 16384], P('section', 'tensor')
The draws below stay inside these ranges and needn't reach their ends.
Inputs may be any that keep to these rules, and one draw needn't show every extreme that they name: `tile_list`: each row lists 128 different tiles; the first tile_count of them are its allowed tiles, the rest are tiles it does not allow. `tile_count`: some row has 128 allowed tiles and some row one. `chosen_token`: each chosen token lies in one of its row's allowed tiles.
All inputs are finite; a program needn't handle non-finite values.
Results may differ from the reference program's by a relative error of at most 0.0035.
Values may be sent and summed in bfloat16 or wider, within the bound.
No kernel may reach another device: no remote copies, remote signals or barrier semaphores. Data moves between devices by JAX's collectives and lax.ppermute only.
A program may use at most 64 MiB of HBM per device.

```python
import math
import jax
import jax.numpy as jnp
from jax import lax

D = 16384
TILE = 128
ROWS = 512
STATES = 512
NTILES = 512
VOCAB = 65536
A_MAX = 128
N_SECTION = 4


def tile_draw(key):
    keys = jax.random.split(jax.random.fold_in(key, 11), 5)
    popular_count = max(NTILES // 16, 1)
    popular = jax.random.permutation(keys[0], NTILES)[:popular_count]
    tile_ids = jnp.arange(NTILES, dtype=jnp.int32)
    is_popular = jnp.any(tile_ids[:, None] == popular[None, :], axis=1).astype(jnp.int32)
    scores = jax.random.randint(keys[1], (ROWS, NTILES), 0, 4096) - 3072 * is_popular[None, :]
    keyed = scores * NTILES + tile_ids[None, :]
    order = jnp.argsort(keyed, axis=1)
    tile_list = order[:, :A_MAX].astype(jnp.int32)
    counts = jax.random.randint(keys[2], (ROWS,), 1, A_MAX + 1).astype(jnp.int32)
    counts = counts.at[0].set(A_MAX).at[1].set(1)
    slot = jax.random.randint(keys[3], (ROWS,), 0, 1 << 20) % counts
    tile_pick = jnp.take_along_axis(tile_list, slot[:, None], axis=1)[:, 0]
    chosen = (tile_pick * TILE + jax.random.randint(keys[4], (ROWS,), 0, TILE)).astype(jnp.int32)
    return (tile_list, counts, chosen)


def draw_tile_list(key, part):
    return tile_draw(key)[0]


def draw_tile_count(key, part):
    return tile_draw(key)[1]


def draw_chosen_token(key, part):
    return tile_draw(key)[2]


def draw_hidden(key, part):
    keys = jax.random.split(jax.random.fold_in(key, 31), 3)
    row_scale = jnp.exp(jax.random.uniform(keys[0], (ROWS,), jnp.float32, 0.0, math.log(10.0)))
    column_scale = jnp.exp(jax.random.uniform(keys[1], (D,), jnp.float32, 0.0, math.log(10.0)))
    values = jax.random.normal(keys[2], (ROWS, D), jnp.float32) * row_scale[:, None] * column_scale[None, :]
    return values.astype(jnp.bfloat16)


def draw_head_weight(key, part):
    keys = jax.random.split(jax.random.fold_in(key, 41), 1)
    spread = 3.0 / math.sqrt(D)
    weight = jax.random.normal(keys[0], (D, VOCAB), jnp.float32) * spread
    return weight.astype(jnp.bfloat16)


def place_ends(values, key, least, top_value):
    place = [jax.random.randint(jax.random.fold_in(key, axis), (), 0, length) for axis, length in enumerate(values.shape)]
    widest = values.shape.index(max(values.shape))
    beside = place[:widest] + [(place[widest] + 1) % values.shape[widest]] + place[widest + 1:]
    return values.at[tuple(place)].set(least).at[tuple(beside)].set(top_value)


def steps_of(key, extent, cuts, low, high):
    def one(dim, parts):
        draws = jax.random.uniform(jax.random.fold_in(jax.random.fold_in(key, 6), dim), (parts,), jnp.float32, low / len(cuts), high / len(cuts))
        return jnp.repeat(jnp.exp(draws), extent[dim] // parts).reshape((-1,) + (1,) * (len(extent) - dim - 1))

    level = one(*cuts[0])
    for cut in cuts[1:]:
        level = level * one(*cut)
    return level


def noise(rng, extent, scale, reach, shards=(), kind=jnp.bfloat16):
    loudness = steps_of(rng, extent, shards, -0.22, 0.18) if shards else 1.0
    drawn = jax.random.normal(rng, extent, jnp.float32) * scale * loudness
    return jnp.minimum(jnp.maximum(drawn, -reach), reach).astype(kind)


def setup_inputs(seed: int = 0) -> dict:
    arg_keys = jax.random.split(jax.random.key(seed), 10)
    return {
        "hidden": draw_hidden(jax.random.fold_in(arg_keys[9], 71), 0),
        "norm_gain": jnp.clip(jnp.exp(math.log(3.0) - 2.3025851 * jax.random.uniform(arg_keys[1], (D,), jnp.float32) ** steps_of(arg_keys[1], (D,), ((0, 64),), -0.2, 0.2)), 0.3, 3.0),
        "head_weight": draw_head_weight(jax.random.fold_in(arg_keys[9], 71), 0),
        "tile_list": draw_tile_list(jax.random.fold_in(arg_keys[9], 71), 0),
        "tile_count": draw_tile_count(jax.random.fold_in(arg_keys[9], 71), 0),
        "chosen_token": draw_chosen_token(jax.random.fold_in(arg_keys[9], 71), 0),
        "chosen_embed": noise(arg_keys[6], (ROWS, D), 1.0, 6.0, ((0, 4), (1, 64))),
        "stack_state": place_ends(jax.random.randint(arg_keys[7], (ROWS,), 0, STATES), jax.random.fold_in(arg_keys[7], 1), 0, STATES - 1).astype(jnp.int32),
        "state_table": noise(arg_keys[8], (STATES, D), 1.0, 6.0, ((1, 64),)),
    }


EPSILON = 1e-05

def reference(hidden, norm_gain, head_weight, tile_list, tile_count, chosen_token, chosen_embed, stack_state, state_table):
    widened = hidden.astype(jnp.float32)
    mean_square = lax.optimization_barrier(jnp.mean(widened * widened, axis=1, keepdims=True))
    normed = (widened * lax.rsqrt(mean_square + EPSILON) * norm_gain[None, :]).astype(jnp.bfloat16)
    logits = jnp.dot(normed, head_weight, preferred_element_type=jnp.float32)
    tile_ids = jnp.arange(NTILES, dtype=jnp.int32)
    live_slot = jnp.arange(A_MAX, dtype=jnp.int32)[None, :] < tile_count[:, None]
    matches = (tile_list[:, :, None] == tile_ids[None, None, :]) & live_slot[:, :, None]
    allowed = jnp.any(matches, axis=1)
    blocks = logits.reshape(ROWS, NTILES, TILE)
    allowed_mask = jnp.broadcast_to(allowed[:, :, None], blocks.shape)
    row_top = lax.optimization_barrier(jnp.max(jnp.where(allowed_mask, blocks, -jnp.inf), axis=(1, 2)))
    shifted = jnp.where(allowed_mask, blocks - row_top[:, None, None], -jnp.inf)
    totals = lax.optimization_barrier(jnp.sum(jnp.exp(shifted), axis=(1, 2)))
    normalizer = row_top + jnp.log(totals)
    picked = jnp.take_along_axis(logits, chosen_token[:, None].astype(jnp.int32), axis=1)[:, 0]
    log_prob = picked - normalizer
    states = jnp.arange(STATES, dtype=jnp.int32)
    one_hot = (stack_state[:, None] == states[None, :]).astype(jnp.bfloat16)
    state_rows = jnp.dot(one_hot, state_table, preferred_element_type=jnp.float32)
    merged = (chosen_embed.astype(jnp.float32) + state_rows).astype(jnp.bfloat16)
    next_input = jnp.roll(merged, ROWS // N_SECTION, axis=0)
    return (log_prob, normalizer, next_input)
```

```python
import jax
import jax.numpy as jnp
from jax import lax
from jax.experimental import pallas as pl
from jax.experimental.pallas import tpu as pltpu
from jax.sharding import Mesh, PartitionSpec as P

D = 16384
TILE = 128
EPSILON = 1e-05
NEG = float(jnp.finfo(jnp.float32).min)

NX, NY, NZ = 4, 4, 8
RA, RB, RC = 32, 48, 48
UNIT = 256
QUAD = (0, 1, -1, 2)
DZ = (0, 1, -1, 2, 3, 4, -3, -2)


def shifted(value, axis, steps):
    count = lax.axis_size(axis)
    pairs = [(source, (source + steps) % count) for source in range(count)]
    return lax.ppermute(value, axis, pairs)


def swapped(value, axis, bit):
    count = lax.axis_size(axis)
    return lax.ppermute(value, axis, [(source, source ^ bit) for source in range(count)])


def from_offset(value, axis, offset):
    return shifted(value, axis, -offset)


def quad_gather(value, axis):
    parts = [value] + [from_offset(value, axis, offset) for offset in QUAD[1:]]
    return jnp.stack(parts, axis=0)


def quad_ring(value, axis):
    low = from_offset(value, axis, -1)
    high = from_offset(value, axis, 1)
    low_far = from_offset(low[:2], axis, -1)
    high_far = from_offset(high[2:], axis, 1)
    return value, high, low, low_far, high_far


def oct_ring(value, axis):
    low = [value]
    high = [value]
    for _ in range(3):
        low.append(from_offset(low[-1], axis, -1))
        high.append(from_offset(high[-1], axis, 1))
    low_far = from_offset(low[-1][:2], axis, -1)
    high_far = from_offset(high[-1][2:], axis, 1)
    return [value] + high[1:] + low[1:] + [low_far, high_far]


def oct_gather(value, axis):
    up = from_offset(value, axis, 1)
    down = from_offset(value, axis, -1)
    three = from_offset(jnp.stack([down, value, up]), axis, 3)
    two = from_offset(jnp.stack([value, up]), axis, -3)
    return jnp.concatenate([jnp.stack([value, up, down]), three, two], axis=0)


def logits_kernel(place, *refs):
    a_refs, b_refs, c_refs = refs[0:9], refs[9:14], refs[14:19]
    w_own, w_far, gains = refs[19:22]
    own_out, send_out, ss_out = refs[22:25]
    acc_own, acc_far, acc_ss, a_all = refs[25:29]
    x, y, z = place[0], place[1], place[2]

    for k, dz in enumerate(DZ):
        if dz == 4:
            a_all[k, 0:2] = a_refs[7][...]
            a_all[k, 2:4] = a_refs[8][...]
        else:
            a_all[k] = a_refs[(0, 1, 2, 3, -1, -2, -3).index(dz)][...]
    acc_own[...] = jnp.zeros_like(acc_own)
    acc_far[...] = jnp.zeros_like(acc_far)
    acc_ss[...] = jnp.zeros_like(acc_ss)

    def b_block(j, k):
        far = b_refs[3] if j < 2 else b_refs[4]
        pieces = [b_refs[0][j, k], b_refs[1][j, k], b_refs[2][j, k], far[j % 2, k]]
        return jnp.concatenate(pieces, axis=0)

    def c_block(j, k):
        if j < 3:
            pieces = [c_refs[j][i, k] for i in range(4)]
        else:
            pieces = [c_refs[3][0, k], c_refs[3][1, k], c_refs[4][0, k], c_refs[4][1, k]]
        return jnp.concatenate(pieces, axis=0)

    @pl.loop(0, NZ)
    def step(k):
        dz = jnp.where(k == 0, 0, jnp.where(k == 1, 1, jnp.where(k == 2, -1, jnp.where(k < 6, k - 1, k - 9))))
        lhs = []
        own = []
        far = []
        squares = None
        for j, dy in enumerate(QUAD):
            block = jnp.concatenate(
                [a_all[k, j].reshape(NX * RA, UNIT), b_block(j, k), c_block(j, k)], axis=0
            ).astype(jnp.float32)
            wide = block * block
            term = wide[:, :128] + wide[:, 128:]
            squares = term if squares is None else squares + term
            gain = gains[j, k].astype(jnp.float32)
            scaled = block * (gain[0:1] + gain[1:2])
            at = lax.rem(y + dy + NY, NY) * NZ + lax.rem(z + dz + NZ, NZ)
            rows = pl.ds(pl.multiple_of(at * UNIT, UNIT), UNIT)
            lhs.append(scaled.astype(jnp.bfloat16))
            own.append(w_own[rows, :])
            far.append(w_far[rows, :])
        left = jnp.concatenate(lhs, axis=1)
        acc_own[...] += jnp.dot(left, jnp.concatenate(own, axis=0), preferred_element_type=jnp.float32)
        acc_far[...] += jnp.dot(left, jnp.concatenate(far, axis=0), preferred_element_type=jnp.float32)
        acc_ss[...] += squares

    base = 0
    for count, offset in ((RA, 0), (RB, RA), (RC, RA + RB)):
        for j, dx in enumerate(QUAD):
            source = pl.ds(base + j * count, count)
            at = lax.rem(x + dx + NX, NX) * (RA + RB + RC) + offset
            target = pl.ds(pl.multiple_of(at, 16), count)
            own_out[target, :] = acc_own[source, :]
            send_out[target, 0:256] = acc_far[source, :]
            send_out[target, 256:384] = acc_ss[source, :]
            ss_out[target, :] = acc_ss[source, :]
        base += NX * count


def stats_kernel(own, received, squares, allowed, column, out):
    total = jnp.sum(squares[...] + received[:, 256:384], axis=1, keepdims=True)
    factor = lax.rsqrt(total / D + EPSILON)
    logits = ((own[...] + received[:, 0:256]) * factor).T
    live = jnp.concatenate([allowed[0:1, :] + jnp.zeros((TILE, 512), jnp.float32),
                            allowed[1:2, :] + jnp.zeros((TILE, 512), jnp.float32)], axis=0) > 0
    masked = jnp.where(live, logits, NEG)
    top = jnp.max(masked, axis=0, keepdims=True)
    terms = jnp.sum(jnp.where(live, jnp.exp(masked - top), 0.0), axis=0, keepdims=True)
    index = lax.broadcasted_iota(jnp.int32, (256, 512), 0)
    picked = jnp.sum(jnp.where(index == column[...], logits, 0.0), axis=0, keepdims=True)
    out[...] = jnp.concatenate([top, terms, picked, jnp.zeros((5, 512), jnp.float32)], axis=0)


def merged_stats(stats):
    top = stats[0][0]
    for other in stats[1:]:
        top = jnp.maximum(top, other[0])
    terms = 0.0
    picked = 0.0
    for other in stats:
        terms = terms + other[1] * jnp.exp(other[0] - top)
        picked = picked + other[2]
    return jnp.stack([top, terms, picked])


def shards(
    hidden,
    norm_gain,
    head_weight,
    tile_list,
    tile_count,
    chosen_token,
    chosen_embed,
    stack_state,
    state_table,
):
    x, y, z, c = (lax.axis_index(name) for name in "xyzc")
    coarse = norm_gain.astype(jnp.bfloat16)
    fine = (norm_gain - coarse.astype(jnp.float32)).astype(jnp.bfloat16)
    pad = jnp.zeros((6, UNIT), jnp.bfloat16)
    gain_rows = jnp.concatenate([coarse[None], fine[None], pad])
    part_a, part_bc = hidden[:RA], jnp.concatenate([gain_rows, hidden[RA:]])
    in_z = oct_gather(part_bc, "z")
    a_plane = quad_gather(quad_gather(part_a, "x"), "y")
    b_plane = quad_gather(in_z[:, :8 + RB], "y")
    c_plane = quad_gather(in_z[:, 8 + RB:], "x")
    gains, b_plane = b_plane[:, :, :8], b_plane[:, :, 8:]
    a_blocks = oct_ring(a_plane, "z")
    b_blocks = quad_ring(b_plane, "x")
    c_blocks = quad_ring(c_plane, "y")

    halves = head_weight.reshape(32, 2, UNIT, 256)
    w_own = lax.dynamic_index_in_dim(halves, c, 1, keepdims=False).reshape(D // 2, 256)
    w_give = lax.dynamic_index_in_dim(halves, 1 - c, 1, keepdims=False).reshape(D // 2, 256)
    w_far = swapped(w_give, "c", 1)

    states = jnp.arange(state_table.shape[0], dtype=jnp.int32)
    one_hot = (stack_state[:, None] == states[None, :]).astype(jnp.bfloat16)
    state_rows = jnp.dot(one_hot, state_table, preferred_element_type=jnp.float32)
    merged = (chosen_embed.astype(jnp.float32) + state_rows).astype(jnp.bfloat16)
    next_input = shifted(merged, "x", 1)

    device = ((x * NY + y) * NZ + z) * 2 + c
    own_tiles = device * 2 + jnp.arange(2, dtype=jnp.int32)
    live_slot = jnp.arange(tile_list.shape[1], dtype=jnp.int32)[None, :] < tile_count[:, None]
    matches = (tile_list[None] == own_tiles[:, None, None]) & live_slot[None]
    allowed = jnp.any(matches, axis=2).astype(jnp.float32)
    column = (chosen_token - device * 256)[None, :]

    place = jnp.stack([x, y, z]).astype(jnp.int32)
    vmem = pl.BlockSpec(memory_space=pltpu.VMEM)
    own, send, squares = pl.pallas_call(
        logits_kernel,
        out_shape=(
            jax.ShapeDtypeStruct((512, 256), jnp.float32),
            jax.ShapeDtypeStruct((512, 384), jnp.float32),
            jax.ShapeDtypeStruct((512, 128), jnp.float32),
        ),
        in_specs=[pl.BlockSpec(memory_space=pltpu.SMEM)] + [vmem] * 22,
        out_specs=(vmem, vmem, vmem),
        scratch_shapes=[
            pltpu.VMEM((512, 256), jnp.float32),
            pltpu.VMEM((512, 256), jnp.float32),
            pltpu.VMEM((512, 128), jnp.float32),
            pltpu.VMEM((NZ, NY, NX, RA, UNIT), jnp.bfloat16),
        ],
        compiler_params=pltpu.CompilerParams(vmem_limit_bytes=32 << 20),
        cost_estimate=pl.CostEstimate(flops=2 * 512 * 8192 * 512, bytes_accessed=16 << 20, transcendentals=0),
    )(place, *a_blocks, *b_blocks, *c_blocks, w_own, w_far, gains)
    received = swapped(send, "c", 1)
    stats = pl.pallas_call(
        stats_kernel,
        out_shape=jax.ShapeDtypeStruct((8, 512), jnp.float32),
        in_specs=[vmem] * 5,
        out_specs=vmem,
        compiler_params=pltpu.CompilerParams(vmem_limit_bytes=12 << 20),
    )(own, received, squares, allowed, column)
    stats = stats[:3]
    stats = merged_stats([stats, swapped(stats, "c", 1)])
    for bit in (1, 2, 4):
        stats = merged_stats([stats, swapped(stats, "z", bit)])
    for axis in ("y", "x"):
        stats = merged_stats([stats] + [from_offset(stats, axis, offset) for offset in QUAD[1:]])
    normalizer = stats[0] + jnp.log(stats[1])
    log_prob = stats[2] - normalizer
    return (log_prob, normalizer, next_input)


def solution(mesh):
    fine = Mesh(mesh.devices.reshape(NX, NY, NZ, 2), ("x", "y", "z", "c"))
    rest = ("y", "z", "c")
    placed = (
        P("x", rest),
        P(rest),
        P(None, ("x", "y", "z", "c")),
        P(),
        P(),
        P(),
        P("x", rest),
        P("x"),
        P(None, rest),
    )
    return jax.shard_map(
        shards,
        mesh=fine,
        in_specs=placed,
        out_specs=(P(), P(), P("x", rest)),
        check_vma=False,
    )
```

```python
import jax
import jax.numpy as jnp
from jax import lax
from jax.experimental import pallas as pl
from jax.experimental.pallas import tpu as pltpu
from jax.sharding import Mesh, PartitionSpec as P


D = 16384
TILE = 128
EPSILON = 1e-05
NEG = float(jnp.finfo(jnp.float32).min)

NX, NY, NZ = 4, 4, 8
RA, RB, RC = 32, 48, 48
UNIT = 256
EXTRA = 8
QUAD = (0, 1, -1, 2)
DZ = (0, 1, -1, 2, 3, 4, -3, -2)


def shifted(value, axis, steps):
    count = lax.axis_size(axis)
    pairs = [(source, (source + steps) % count) for source in range(count)]
    return lax.ppermute(value, axis, pairs)


def swapped(value, axis, bit):
    count = lax.axis_size(axis)
    return lax.ppermute(value, axis, [(source, source ^ bit) for source in range(count)])


def from_offset(value, axis, offset):
    return shifted(value, axis, -offset)


def oct_merged(stats, axis):
    up = from_offset(stats, axis, 1)
    down = from_offset(stats, axis, -1)
    three = merged_stats([down, stats, up])
    two = merged_stats([stats, up])
    return merged_stats([three, from_offset(three, axis, 3), from_offset(two, axis, -3)])


def quad_sent(value, axis):
    return [value] + [from_offset(value, axis, QUAD[i]) for i in (1, 2, 3)]


def halves_of(parts):
    return jnp.stack(parts[:2]), jnp.stack(parts[2:])


def ring_of_four(halves, axis):
    first, second = halves
    low_first = from_offset(first, axis, -1)
    high_second = from_offset(second, axis, 1)
    low_second = from_offset(second, axis, -1)
    high_first = from_offset(first, axis, 1)
    far_first = from_offset(low_first, axis, -1)
    far_second = from_offset(high_second, axis, 1)
    return first, second, high_first, high_second, low_first, low_second, far_first, far_second


def gathered(part_a, part_bc):
    up = from_offset(part_bc, "z", 1)
    down = from_offset(part_bc, "z", -1)
    a_line = jnp.stack(quad_sent(part_a, "x"))
    three = from_offset(jnp.stack([down, part_bc, up]), "z", 3)
    two = from_offset(jnp.stack([part_bc, up]), "z", -3)
    a_plane = jnp.stack(quad_sent(a_line, "y"))
    in_z = jnp.concatenate([jnp.stack([part_bc, up, down]), three, two], axis=0)
    c_halves = halves_of(quad_sent(in_z[:, RB:], "x"))
    b_halves = halves_of(quad_sent(in_z[:, :RB], "y"))
    c_blocks = ring_of_four(c_halves, "y")
    b_blocks = ring_of_four(b_halves, "x")
    low = [from_offset(a_plane, "z", -1)]
    high = [from_offset(a_plane, "z", 1)]
    for _ in range(2):
        low.append(from_offset(low[-1], "z", -1))
        high.append(from_offset(high[-1], "z", 1))
    a_far = from_offset(low[2][:2], "z", -1), from_offset(high[2][2:], "z", 1)
    return (a_plane, *high, *low, *a_far), b_blocks, c_blocks


def fetch_kernel(place, w_own, w_far, out, sem):
    y, z, c = place[1], place[2], place[3]

    def weight_copies(k):
        dz = jnp.where(k < 2, k, jnp.where(k == 2, -1, jnp.where(k < 6, k - 1, k - 9)))
        copies = []
        for j, dy in enumerate(QUAD):
            at = lax.rem(y + dy + NY, NY) * NZ + lax.rem(z + dz + NZ, NZ)
            rows = pl.ds(pl.multiple_of((at * 2 + c) * UNIT, UNIT), UNIT)
            for side, ref in enumerate((w_own, w_far)):
                target = out.at[k, side, pl.ds(j * UNIT, UNIT), :]
                copies.append(pltpu.make_async_copy(ref.at[rows, :], target, sem.at[k, side, j]))
        return copies

    @pl.loop(0, NZ)
    def start(k):
        for copy in weight_copies(k):
            copy.start()

    @pl.loop(0, NZ)
    def wait(k):
        for copy in weight_copies(k):
            copy.wait()


def logits_kernel(place, *refs):
    a_refs, b_refs, c_refs = refs[0:9], refs[9:17], refs[17:25]
    weights = refs[25]
    own_out, send_out, ss_out = refs[26:29]
    acc, a_all = refs[29:31]
    x = place[0]

    for k, dz in enumerate(DZ):
        if dz == 4:
            a_all[k, 0:2] = a_refs[7][...]
            a_all[k, 2:4] = a_refs[8][...]
        else:
            a_all[k] = a_refs[(0, 1, 2, 3, -1, -2, -3).index(dz)][...]
    acc[...] = jnp.zeros_like(acc)

    @pl.loop(0, NZ)
    def step(k):
        columns = []
        for j in range(NY):
            pieces = [a_all[k, j].reshape(NX * RA, UNIT)]
            pieces += [b_refs[2 * i + j // 2][j % 2, k] for i in range(NX)]
            pieces += [c_refs[2 * j + i // 2][i % 2, k, 0:RC] for i in range(NX)]
            columns.append(jnp.concatenate(pieces, axis=0))
        left = jnp.concatenate(columns, axis=1)
        acc[0] += jnp.dot(left, weights[k, 0], preferred_element_type=jnp.float32)
        acc[1] += jnp.dot(left, weights[k, 1], preferred_element_type=jnp.float32)

    section = lax.broadcasted_iota(jnp.int32, (8, 128), 0)
    sums = jnp.zeros((8, 128), jnp.float32)
    for i, dx in enumerate(QUAD):
        total = jnp.zeros((EXTRA, UNIT), jnp.float32)
        for j in range(NY):
            for k in range(NZ):
                total = total + c_refs[2 * j + i // 2][i % 2, k, RC:RC + EXTRA].astype(jnp.float32)
        squares = total[0:1, 0:128] + total[0:1, 128:256]
        sums = jnp.where(section == lax.rem(x + dx + NX, NX), squares, sums)
    ss_out[...] = sums
    send_out[512:520, 0:128] = sums
    send_out[512:520, 128:256] = sums
    base = 0
    for count, offset in ((RA, 0), (RB, RA), (RC, RA + RB)):
        for i, dx in enumerate(QUAD):
            source = pl.ds(base + i * count, count)
            at = lax.rem(x + dx + NX, NX) * (RA + RB + RC) + offset
            target = pl.ds(pl.multiple_of(at, 16), count)
            own_out[target, :] = acc[0, source, :]
            send_out[target, :] = acc[1, source, :]
        base += NX * count


def stats_kernel(own, received, squares, allowed, column, out):
    sums = squares[...] + received[512:520, 0:128]
    total = jnp.concatenate([sums[i:i + 1] for i in range(NX)], axis=1)
    factor = lax.rsqrt(total / D + EPSILON)
    logits = (own[...] + received[0:512, :]).T * factor
    live = jnp.concatenate([allowed[0:1, :] + jnp.zeros((TILE, 512), jnp.float32),
                            allowed[1:2, :] + jnp.zeros((TILE, 512), jnp.float32)], axis=0) > 0
    masked = jnp.where(live, logits, NEG)
    top = jnp.max(masked, axis=0, keepdims=True)
    terms = jnp.sum(jnp.where(live, jnp.exp(masked - top), 0.0), axis=0, keepdims=True)
    index = lax.broadcasted_iota(jnp.int32, (256, 512), 0)
    picked = jnp.sum(jnp.where(index == column[...], logits, 0.0), axis=0, keepdims=True)
    out[...] = jnp.concatenate([top, terms, picked, jnp.zeros((5, 512), jnp.float32)], axis=0)


def merged_stats(stats):
    top = stats[0][0]
    for other in stats[1:]:
        top = jnp.maximum(top, other[0])
    terms = 0.0
    picked = 0.0
    for other in stats:
        terms = terms + other[1] * jnp.exp(other[0] - top)
        picked = picked + other[2]
    return jnp.stack([top, terms, picked])


def in_hbm(value):
    return pltpu.with_memory_space_constraint(value, pltpu.HBM)


def head_step(
    hidden,
    norm_gain,
    head_weight,
    tile_list,
    tile_count,
    chosen_token,
    chosen_embed,
    stack_state,
    state_table,
):
    x, y, z, c = (lax.axis_index(name) for name in "xyzc")
    wide = hidden.astype(jnp.float32)
    squares = jnp.sum(wide * wide, axis=1)
    scaled = (wide * norm_gain[None, :]).astype(jnp.bfloat16)
    coarse = lax.reduce_precision(squares, 8, 7)
    carried = jnp.concatenate([coarse, squares - coarse]).astype(jnp.bfloat16)[None]
    pad = jnp.zeros((EXTRA - 1, UNIT), jnp.bfloat16)
    part_a, part_bc = scaled[:RA], jnp.concatenate([scaled[RA:], carried, pad])
    a_blocks, b_blocks, c_blocks = gathered(part_a, part_bc)
    w_far = swapped(head_weight, "c", 1)

    states = jnp.arange(state_table.shape[0], dtype=jnp.int32)
    one_hot = (stack_state[:, None] == states[None, :]).astype(jnp.bfloat16)
    state_rows = jnp.dot(one_hot, state_table, preferred_element_type=jnp.float32)
    merged = (chosen_embed.astype(jnp.float32) + state_rows).astype(jnp.bfloat16)
    next_input = shifted(merged, "x", 1)

    device = ((x * NY + y) * NZ + z) * 2 + c
    own_tiles = device * 2 + jnp.arange(2, dtype=jnp.int32)
    live_slot = jnp.arange(tile_list.shape[1], dtype=jnp.int32)[None, :] < tile_count[:, None]
    matches = (tile_list[None] == own_tiles[:, None, None]) & live_slot[None]
    allowed = jnp.any(matches, axis=2).astype(jnp.float32)
    column = (chosen_token - device * 256)[None, :]

    place = jnp.stack([x, y, z, c]).astype(jnp.int32)
    vmem = pl.BlockSpec(memory_space=pltpu.VMEM)
    raw = pl.BlockSpec(memory_space=pltpu.HBM)
    smem = pl.BlockSpec(memory_space=pltpu.SMEM)
    weights = pl.pallas_call(
        fetch_kernel,
        out_shape=jax.ShapeDtypeStruct((NZ, 2, NY * UNIT, 256), jnp.bfloat16),
        in_specs=[smem, raw, raw],
        out_specs=vmem,
        scratch_shapes=[pltpu.SemaphoreType.DMA((NZ, 2, NY))],
        compiler_params=pltpu.CompilerParams(vmem_limit_bytes=9 << 20),
        cost_estimate=pl.CostEstimate(flops=0, bytes_accessed=8 << 20, transcendentals=0),
    )(place, in_hbm(head_weight), in_hbm(w_far))
    own, send, squares = pl.pallas_call(
        logits_kernel,
        out_shape=(
            jax.ShapeDtypeStruct((512, 256), jnp.float32),
            jax.ShapeDtypeStruct((520, 256), jnp.float32),
            jax.ShapeDtypeStruct((8, 128), jnp.float32),
        ),
        in_specs=[smem] + [vmem] * 26,
        out_specs=(vmem, vmem, vmem),
        scratch_shapes=[
            pltpu.VMEM((2, 512, 256), jnp.float32),
            pltpu.VMEM((NZ, NY, NX, RA, UNIT), jnp.bfloat16),
        ],
        compiler_params=pltpu.CompilerParams(vmem_limit_bytes=24 << 20),
        cost_estimate=pl.CostEstimate(flops=2 * 512 * 8192 * 512, bytes_accessed=16 << 20, transcendentals=0),
    )(place, *a_blocks, *b_blocks, *c_blocks, weights)
    received = swapped(send, "c", 1)
    stats = pl.pallas_call(
        stats_kernel,
        out_shape=jax.ShapeDtypeStruct((8, 512), jnp.float32),
        in_specs=[vmem] * 5,
        out_specs=vmem,
        compiler_params=pltpu.CompilerParams(vmem_limit_bytes=8 << 20),
    )(own, received, squares, allowed, column)
    stats = stats[:3]
    stats = merged_stats([stats, swapped(stats, "c", 1)])
    stats = oct_merged(stats, "z")
    for axis in ("y", "x"):
        stats = merged_stats([stats] + [from_offset(stats, axis, offset) for offset in QUAD[1:]])
    normalizer = stats[0] + jnp.log(stats[1])
    log_prob = stats[2] - normalizer
    return (log_prob, normalizer, next_input)


def solution(mesh):
    fine = Mesh(mesh.devices.reshape(NX, NY, NZ, 2), ("x", "y", "z", "c"))
    rest = ("y", "z", "c")
    placed = (
        P("x", rest),
        P(rest),
        P(None, ("x", "y", "z", "c")),
        P(),
        P(),
        P(),
        P("x", rest),
        P("x"),
        P(None, rest),
    )
    return jax.shard_map(
        head_step,
        mesh=fine,
        in_specs=placed,
        out_specs=(P(), P(), P("x", rest)),
        check_vma=False,
    )
```

```python
import jax
import jax.numpy as jnp
from jax import lax
from jax.experimental import pallas as pl
from jax.experimental.pallas import tpu as pltpu
from jax.sharding import Mesh, PartitionSpec as P


D = 16384
TILE = 128
EPSILON = 1e-05
NEG = float(jnp.finfo(jnp.float32).min)

NX, NY, NZ = 4, 4, 8
RA, RB, RC = 32, 48, 48
UNIT = 256
EXTRA = 8
QUAD = (0, 1, -1, 2)
DZ = (0, 1, -1, 2, 3, 4, -3, -2)


def shifted(value, axis, steps):
    count = lax.axis_size(axis)
    pairs = [(source, (source + steps) % count) for source in range(count)]
    return lax.ppermute(value, axis, pairs)


def swapped(value, axis, bit):
    count = lax.axis_size(axis)
    return lax.ppermute(value, axis, [(source, source ^ bit) for source in range(count)])


def from_offset(value, axis, offset):
    return shifted(value, axis, -offset)


def oct_merged(stats, axis):
    up = from_offset(stats, axis, 1)
    down = from_offset(stats, axis, -1)
    three = merged_stats([down, stats, up])
    two = merged_stats([stats, up])
    return merged_stats([three, from_offset(three, axis, 3), from_offset(two, axis, -3)])


def quad_sent(value, axis):
    return [value] + [from_offset(value, axis, QUAD[i]) for i in (1, 2, 3)]


def halves_of(parts):
    return jnp.stack(parts[:2]), jnp.stack(parts[2:])


def ring_of_four(halves, axis):
    first, second = halves
    low_first = from_offset(first, axis, -1)
    high_second = from_offset(second, axis, 1)
    low_second = from_offset(second, axis, -1)
    high_first = from_offset(first, axis, 1)
    far_first = from_offset(low_first, axis, -1)
    far_second = from_offset(high_second, axis, 1)
    return first, second, high_first, high_second, low_first, low_second, far_first, far_second


def gathered(part_a, part_bc):
    up = from_offset(part_bc, "z", 1)
    down = from_offset(part_bc, "z", -1)
    a_line = jnp.stack(quad_sent(part_a, "x"))
    three = jnp.stack([down, part_bc, up])
    two = jnp.stack([part_bc, up])
    three = from_offset(three, "z", 3)
    two = from_offset(two, "z", -3)
    a_plane = jnp.stack(quad_sent(a_line, "y"))
    in_z = jnp.concatenate([jnp.stack([part_bc, up, down]), three, two], axis=0)
    c_halves = halves_of(quad_sent(in_z[:, RB:], "x"))
    b_halves = halves_of(quad_sent(in_z[:, :RB], "y"))
    c_blocks = ring_of_four(c_halves, "y")
    b_blocks = ring_of_four(b_halves, "x")
    low = [from_offset(a_plane, "z", -1)]
    high = [from_offset(a_plane, "z", 1)]
    for _ in range(2):
        low.append(from_offset(low[-1], "z", -1))
        high.append(from_offset(high[-1], "z", 1))
    a_far = from_offset(low[2][:2], "z", -1), from_offset(high[2][2:], "z", 1)
    return (a_plane, *high, *low, *a_far), b_blocks, c_blocks


def fetch_kernel(place, w_own, w_far, out, sem):
    y, z, c = place[1], place[2], place[3]

    def weight_copies(k):
        dz = jnp.where(k < 2, k, jnp.where(k == 2, -1, jnp.where(k < 6, k - 1, k - 9)))
        copies = []
        for j, dy in enumerate(QUAD):
            at = lax.rem(y + dy + NY, NY) * NZ + lax.rem(z + dz + NZ, NZ)
            rows = pl.ds(pl.multiple_of((at * 2 + c) * UNIT, UNIT), UNIT)
            for side, ref in enumerate((w_own, w_far)):
                target = out.at[k, side, pl.ds(j * UNIT, UNIT), :]
                copies.append(pltpu.make_async_copy(ref.at[rows, :], target, sem.at[k, side, j]))
        return copies

    @pl.loop(0, NZ)
    def start(k):
        for copy in weight_copies(k):
            copy.start()

    @pl.loop(0, NZ)
    def wait(k):
        for copy in weight_copies(k):
            copy.wait()


def logits_kernel(place, *refs):
    a_refs, b_refs, c_refs = refs[0:9], refs[9:17], refs[17:25]
    weights = refs[25]
    own_out, send_out, ss_out = refs[26:29]
    acc, a_all = refs[29:31]
    x = place[0]

    for k, dz in enumerate(DZ):
        if dz == 4:
            a_all[k, 0:2] = a_refs[7][...]
            a_all[k, 2:4] = a_refs[8][...]
        else:
            a_all[k] = a_refs[(0, 1, 2, 3, -1, -2, -3).index(dz)][...]
    acc[...] = jnp.zeros_like(acc)

    @pl.loop(0, NZ)
    def step(k):
        columns = []
        for j in range(NY):
            pieces = [a_all[k, j].reshape(NX * RA, UNIT)]
            pieces += [b_refs[2 * i + j // 2][j % 2, k] for i in range(NX)]
            pieces += [c_refs[2 * j + i // 2][i % 2, k, 0:RC] for i in range(NX)]
            columns.append(jnp.concatenate(pieces, axis=0))
        left = jnp.concatenate(columns, axis=1)
        acc[0] += jnp.dot(left, weights[k, 0], preferred_element_type=jnp.float32)
        acc[1] += jnp.dot(left, weights[k, 1], preferred_element_type=jnp.float32)

    section = lax.broadcasted_iota(jnp.int32, (8, 128), 0)
    sums = jnp.zeros((8, 128), jnp.float32)
    for i, dx in enumerate(QUAD):
        total = jnp.zeros((EXTRA, UNIT), jnp.float32)
        for j in range(NY):
            for k in range(NZ):
                total = total + c_refs[2 * j + i // 2][i % 2, k, RC:RC + EXTRA].astype(jnp.float32)
        squares = total[0:1, 0:128] + total[0:1, 128:256]
        sums = jnp.where(section == lax.rem(x + dx + NX, NX), squares, sums)
    ss_out[...] = sums
    send_out[512:520, 0:128] = sums
    send_out[512:520, 128:256] = sums
    base = 0
    for count, offset in ((RA, 0), (RB, RA), (RC, RA + RB)):
        for i, dx in enumerate(QUAD):
            source = pl.ds(base + i * count, count)
            at = lax.rem(x + dx + NX, NX) * (RA + RB + RC) + offset
            target = pl.ds(pl.multiple_of(at, 16), count)
            own_out[target, :] = acc[0, source, :]
            send_out[target, :] = acc[1, source, :]
        base += NX * count


def stats_kernel(own, received, squares, allowed, column, out):
    sums = squares[...] + received[512:520, 0:128]
    total = jnp.concatenate([sums[i:i + 1] for i in range(NX)], axis=1)
    factor = lax.rsqrt(total / D + EPSILON)
    logits = (own[...] + received[0:512, :]).T * factor
    live = jnp.concatenate([allowed[0:1, :] + jnp.zeros((TILE, 512), jnp.float32),
                            allowed[1:2, :] + jnp.zeros((TILE, 512), jnp.float32)], axis=0) > 0
    masked = jnp.where(live, logits, NEG)
    top = jnp.max(masked, axis=0, keepdims=True)
    terms = jnp.sum(jnp.where(live, jnp.exp(masked - top), 0.0), axis=0, keepdims=True)
    index = lax.broadcasted_iota(jnp.int32, (256, 512), 0)
    picked = jnp.sum(jnp.where(index == column[...], logits, 0.0), axis=0, keepdims=True)
    out[...] = jnp.concatenate([top, terms, picked, jnp.zeros((5, 512), jnp.float32)], axis=0)


def merged_stats(stats):
    top = stats[0][0]
    for other in stats[1:]:
        top = jnp.maximum(top, other[0])
    terms = 0.0
    picked = 0.0
    for other in stats:
        terms = terms + other[1] * jnp.exp(other[0] - top)
        picked = picked + other[2]
    return jnp.stack([top, terms, picked])


def in_hbm(value):
    return pltpu.with_memory_space_constraint(value, pltpu.HBM)


def head_step(
    hidden,
    norm_gain,
    head_weight,
    tile_list,
    tile_count,
    chosen_token,
    chosen_embed,
    stack_state,
    state_table,
):
    x, y, z, c = (lax.axis_index(name) for name in "xyzc")
    wide = hidden.astype(jnp.float32)
    squares = jnp.sum(wide * wide, axis=1)
    scaled = (wide * norm_gain[None, :]).astype(jnp.bfloat16)
    coarse = lax.reduce_precision(squares, 8, 7)
    carried = jnp.concatenate([coarse, squares - coarse]).astype(jnp.bfloat16)[None]
    pad = jnp.zeros((EXTRA - 1, UNIT), jnp.bfloat16)
    part_a, part_bc = scaled[:RA], jnp.concatenate([scaled[RA:], carried, pad])
    a_blocks, b_blocks, c_blocks = gathered(part_a, part_bc)
    w_far = swapped(head_weight, "c", 1)

    states = jnp.arange(state_table.shape[0], dtype=jnp.int32)
    one_hot = (stack_state[:, None] == states[None, :]).astype(jnp.bfloat16)
    state_rows = jnp.dot(one_hot, state_table, preferred_element_type=jnp.float32)
    merged = (chosen_embed.astype(jnp.float32) + state_rows).astype(jnp.bfloat16)
    next_input = shifted(merged, "x", 1)

    device = ((x * NY + y) * NZ + z) * 2 + c
    own_tiles = device * 2 + jnp.arange(2, dtype=jnp.int32)
    live_slot = jnp.arange(tile_list.shape[1], dtype=jnp.int32)[None, :] < tile_count[:, None]
    matches = (tile_list[None] == own_tiles[:, None, None]) & live_slot[None]
    allowed = jnp.any(matches, axis=2).astype(jnp.float32)
    column = (chosen_token - device * 256)[None, :]

    place = jnp.stack([x, y, z, c]).astype(jnp.int32)
    vmem = pl.BlockSpec(memory_space=pltpu.VMEM)
    raw = pl.BlockSpec(memory_space=pltpu.HBM)
    smem = pl.BlockSpec(memory_space=pltpu.SMEM)
    weights = pl.pallas_call(
        fetch_kernel,
        out_shape=jax.ShapeDtypeStruct((NZ, 2, NY * UNIT, 256), jnp.bfloat16),
        in_specs=[smem, raw, raw],
        out_specs=vmem,
        scratch_shapes=[pltpu.SemaphoreType.DMA((NZ, 2, NY))],
        compiler_params=pltpu.CompilerParams(vmem_limit_bytes=9 << 20),
        cost_estimate=pl.CostEstimate(flops=0, bytes_accessed=8 << 20, transcendentals=0),
    )(place, in_hbm(head_weight), in_hbm(w_far))
    own, send, squares = pl.pallas_call(
        logits_kernel,
        out_shape=(
            jax.ShapeDtypeStruct((512, 256), jnp.float32),
            jax.ShapeDtypeStruct((520, 256), jnp.float32),
            jax.ShapeDtypeStruct((8, 128), jnp.float32),
        ),
        in_specs=[smem] + [vmem] * 26,
        out_specs=(vmem, vmem, vmem),
        scratch_shapes=[
            pltpu.VMEM((2, 512, 256), jnp.float32),
            pltpu.VMEM((NZ, NY, NX, RA, UNIT), jnp.bfloat16),
        ],
        compiler_params=pltpu.CompilerParams(vmem_limit_bytes=24 << 20),
        cost_estimate=pl.CostEstimate(flops=2 * 512 * 8192 * 512, bytes_accessed=16 << 20, transcendentals=0),
    )(place, *a_blocks, *b_blocks, *c_blocks, weights)
    received = swapped(send, "c", 1)
    stats = pl.pallas_call(
        stats_kernel,
        out_shape=jax.ShapeDtypeStruct((8, 512), jnp.float32),
        in_specs=[vmem] * 5,
        out_specs=vmem,
        compiler_params=pltpu.CompilerParams(vmem_limit_bytes=8 << 20),
    )(own, received, squares, allowed, column)
    stats = stats[:3]
    stats = merged_stats([stats, swapped(stats, "c", 1)])
    stats = oct_merged(stats, "z")
    plane = NX * NY
    local = jnp.concatenate([stats[0] + jnp.log(stats[1]), stats[2]]).reshape(8, 128)
    copies = jnp.broadcast_to(local[None], (plane, 8, 128))
    every = lax.all_to_all(copies, ("x", "y"), 0, 0, tiled=True)
    logs = every[:, 0:4]
    top = jnp.max(logs, axis=0)
    normalizer = top + jnp.log(jnp.sum(jnp.exp(logs - top[None]), axis=0))
    log_prob = (jnp.sum(every[:, 4:8], axis=0) - normalizer).reshape(512)
    normalizer = normalizer.reshape(512)
    return (log_prob, normalizer, next_input)


def solution(mesh):
    fine = Mesh(mesh.devices.reshape(NX, NY, NZ, 2), ("x", "y", "z", "c"))
    rest = ("y", "z", "c")
    placed = (
        P("x", rest),
        P(rest),
        P(None, ("x", "y", "z", "c")),
        P(),
        P(),
        P(),
        P("x", rest),
        P("x"),
        P(None, rest),
    )
    return jax.shard_map(
        head_step,
        mesh=fine,
        in_specs=placed,
        out_specs=(P(), P(), P("x", rest)),
        check_vma=False,
    )
```
